256 devices in a mesh: seq: 32 (over z, y), head: 8 (over x, core).
Axes of the slice: x: 4, y: 4, z: 8, core: 2. Of those that a mesh axis runs over, the one named last changes fastest.
Arguments:
- query_in: bfloat16 [32768, 32, 128], P(('seq', 'head')), may hold values from -6 to 6
- key_in: bfloat16 [32768, 32, 128], P(('seq', 'head')), may hold values from -6 to 6
- value_in: bfloat16 [32768, 32, 128], P(('seq', 'head')), may hold values from -6 to 6
- grad_out: bfloat16 [32768, 32, 128], P(('seq', 'head')), may hold values from -6 to 6
- log_decay: bfloat16 [32768, 32], P(('seq', 'head')), may hold values from -1 to 0, as said below
Outputs:
- attended: bfloat16 [32768, 32, 128], P(('seq', 'head'))
- grad_query: bfloat16 [32768, 32, 128], P(('seq', 'head'))
- grad_key: bfloat16 [32768, 32, 128], P(('seq', 'head'))
- grad_value: bfloat16 [32768, 32, 128], P(('seq', 'head'))
The draws below stay inside these ranges and needn't reach their ends.
Inputs may be any that keep to these rules, and one draw needn't show every extreme that they name: Every entry of log_decay is negative.
All inputs are finite; a program needn't handle non-finite values.
Results may differ from the reference program's by a relative error of at most 0.007.
Values may be sent and summed in bfloat16 or wider, within the bound.
A program may use at most 128 MiB of HBM per device.

```python
import math
import jax
import jax.numpy as jnp
from jax import lax

HEADS = 32
DH = 128
SEG = 1024
TOKENS = 32768
N_SEQ = 32


def draw_log_decay(key, part):
    parallel_flows = jax.random.split(key, 6)
    share = 0.5
    slowish = jax.random.uniform(parallel_flows[0], (HEADS,)) < share
    slow_rate = jnp.exp(jax.random.uniform(parallel_flows[1], (HEADS,), minval=math.log(0.05), maxval=math.log(0.4))) / TOKENS
    fast_rate = jnp.exp(jax.random.uniform(parallel_flows[2], (HEADS,), minval=math.log(1.0 / 50.0), maxval=math.log(1.0 / 30.0)))
    base_rate = jnp.where(slowish, slow_rate, fast_rate)
    blocks = TOKENS // SEG
    factor = jnp.exp(jax.random.uniform(parallel_flows[3], (blocks, 1, HEADS), minval=-math.log(2.0), maxval=math.log(2.0)))
    forgetting_factors = jnp.broadcast_to(base_rate[None, None, :] * factor, (blocks, SEG, HEADS)).reshape(TOKENS, HEADS)
    piece_locations = jax.random.randint(parallel_flows[4], (2, HEADS), 0, TOKENS)
    shrink_factor = jax.random.uniform(parallel_flows[5], (2, HEADS), minval=0.2, maxval=0.5)
    element_index_within = jnp.arange(TOKENS)[:, None, None]
    contiguous_ranges = jnp.sum(jnp.where(element_index_within == piece_locations[None, :, :], -jnp.log1p(-shrink_factor)[None, :, :], 0.0), axis=1)
    return (-forgetting_factors - contiguous_ranges).astype(jnp.float32).astype(jnp.bfloat16)


def block_levels(key, extent, cuts, smallest, top_value):
    gain, own = 1.0, jax.random.fold_in(key, 6)
    for axis_at, blocks in cuts:
        steps = jnp.exp(jax.random.uniform(jax.random.fold_in(own, axis_at), (blocks,), jnp.float32, smallest / len(cuts), top_value / len(cuts)))
        gain = gain * jnp.repeat(steps, extent[axis_at] // blocks).reshape([-1 if axis == axis_at else 1 for axis in range(len(extent))])
    return gain


def normal_values(stream_key, dims, width, bound, cuts=(), held_as=jnp.bfloat16):
    entries = width * jax.random.normal(stream_key, dims, jnp.float32)
    if cuts:
        entries = entries * block_levels(stream_key, dims, cuts, -0.22, 0.18)
    return jnp.clip(entries, -bound, bound).astype(held_as)


def setup_inputs(seed: int = 0) -> dict:
    seeds = jax.random.split(jax.random.key(seed), 6)
    return {
        "query_in": normal_values(seeds[0], (TOKENS, HEADS, DH), 1.0, 6.0, ((0, 256),)),
        "key_in": normal_values(seeds[1], (TOKENS, HEADS, DH), 1.0, 6.0, ((0, 256),)),
        "value_in": normal_values(seeds[2], (TOKENS, HEADS, DH), 1.0, 6.0, ((0, 256),)),
        "grad_out": normal_values(seeds[3], (TOKENS, HEADS, DH), 1.0, 6.0, ((0, 256),)),
        "log_decay": draw_log_decay(jax.random.fold_in(seeds[5], 71), 0),
    }


precise = lax.Precision.HIGHEST


def rounded(array):
    return lax.optimization_barrier(array.astype(jnp.bfloat16)).astype(jnp.float32)


def single_attention_unit(operands):
    queries, keys_all, values, grads, token_decays = operands
    f32 = jnp.float32
    scaling = 1.0 / DH
    queries = queries.astype(f32)
    keys_all = keys_all.astype(f32)
    values = values.astype(f32)
    grads = grads.astype(f32)
    within = jnp.cumsum(token_decays.astype(f32), axis=1)
    seg_total = within[:, -1]
    to_start = jnp.exp(within)[:, :, None]
    to_end = jnp.exp(seg_total[:, None] - within)[:, :, None]
    causal = jnp.arange(SEG)[:, None] >= jnp.arange(SEG)[None, :]
    gap_log = within[:, :, None] - within[:, None, :]
    decay_mat = jnp.where(causal, jnp.exp(jnp.where(causal, gap_log, 0.0)), 0.0)
    scores = jnp.einsum('ntd,nsd->nts', queries, keys_all, precision=precise)
    attn_w = rounded(scaling * scores * decay_mat)
    intra = jnp.einsum('nts,nsd->ntd', attn_w, values, precision=precise)
    keys_end = rounded(keys_all * to_end)
    values_end = rounded(values * to_end)
    queries_start = rounded(queries * to_start)
    grads_start = rounded(grads * to_start)
    local_kv = rounded(jnp.einsum('ntd,nte->nde', keys_end, values, precision=precise))
    local_qg = rounded(jnp.einsum('ntd,nte->nde', queries_start, grads, precision=precise))
    cum_inc = jnp.cumsum(seg_total)
    cum_exc = cum_inc - seg_total
    ranks = jnp.arange(N_SEQ)
    earlier = ranks[None, :] < ranks[:, None]
    later_on = ranks[None, :] > ranks[:, None]
    w_in = jnp.where(earlier, jnp.exp(jnp.where(earlier, cum_exc[:, None] - cum_inc[None, :], 0.0)), 0.0)
    w_out = jnp.where(later_on, jnp.exp(jnp.where(later_on, cum_exc[None, :] - cum_inc[:, None], 0.0)), 0.0)
    state_in = rounded(jnp.einsum('ji,ide->jde', w_in, local_kv, precision=precise))
    state_out = rounded(jnp.einsum('ji,ide->jde', w_out, local_qg, precision=precise))
    attended = (intra + scaling * jnp.einsum('ntd,nde->nte', queries_start, state_in, precision=precise)).astype(jnp.bfloat16)
    back_raw = jnp.einsum('nte,nse->nts', grads, values, precision=precise)
    back_w = rounded(scaling * back_raw * decay_mat)
    grad_query = (jnp.einsum('nts,nsd->ntd', back_w, keys_all, precision=precise)
                  + scaling * jnp.einsum('nte,nde->ntd', grads_start, state_in, precision=precise)).astype(jnp.bfloat16)
    grad_key = (jnp.einsum('nts,ntd->nsd', back_w, queries, precision=precise)
                + scaling * jnp.einsum('nse,nde->nsd', values_end, state_out, precision=precise)).astype(jnp.bfloat16)
    grad_value = (jnp.einsum('nts,nte->nse', attn_w, grads, precision=precise)
                  + scaling * jnp.einsum('nsd,nde->nse', keys_end, state_out, precision=precise)).astype(jnp.bfloat16)
    return attended, grad_query, grad_key, grad_value


def head_major(array):
    return array.reshape(N_SEQ, SEG, HEADS, DH).transpose(2, 0, 1, 3)


def reference(query_in, key_in, value_in, grad_out, log_decay):
    token_decays = log_decay.reshape(N_SEQ, SEG, HEADS).transpose(2, 0, 1)
    results = lax.map(single_attention_unit, (head_major(query_in), head_major(key_in), head_major(value_in), head_major(grad_out), token_decays))
    return tuple(item.transpose(1, 2, 0, 3).reshape(TOKENS, HEADS, DH) for item in results)
```

```python
import functools

import jax
import jax.numpy as jnp
from jax import lax
from jax.experimental import pallas as pl
from jax.experimental.pallas import tpu as pltpu
from jax.sharding import PartitionSpec as P

precise = lax.Precision.HIGHEST
f32 = jnp.float32
bf16 = jnp.bfloat16


def columns(row, width):
    return jnp.transpose(jnp.broadcast_to(row, (width, row.shape[1])))


def local_states_kernel(q_ref, k_ref, v_ref, g_ref, within_ref, kv_ref, qg_ref):
    width = q_ref.shape[-1]
    length = within_ref.shape[-1]
    col = columns(within_ref[...], width)
    total = col[length - 1 :, :]
    k_end = (k_ref[...].reshape(length, width).astype(f32) * jnp.exp(total - col)).astype(bf16)
    q_start = (q_ref[...].reshape(length, width).astype(f32) * jnp.exp(col)).astype(bf16)
    over_rows = (((0,), (0,)), ((), ()))
    kv_ref[...] = lax.dot_general(
        k_end, v_ref[...].reshape(length, width), over_rows, preferred_element_type=f32
    ).astype(bf16)
    qg_ref[...] = lax.dot_general(
        q_start, g_ref[...].reshape(length, width), over_rows, preferred_element_type=f32
    ).astype(bf16)


def attention_kernel(swap, tile, q_ref, k_ref, v_ref, g_ref, within_ref, in_ref, out_ref, o_ref):
    width = q_ref.shape[-1]
    length = within_ref.shape[-1]
    pieces = q_ref.shape[0]
    scaling = 1.0 / width
    row = within_ref[...]
    col = columns(row, width)
    total = col[length - 1 :, :]
    q = q_ref[...].reshape(length, width)
    k = k_ref[...].reshape(length, width)
    v = v_ref[...].reshape(length, width)
    g = g_ref[...].reshape(length, width)
    count = length // tile
    cut = lambda x, i: x[i * tile : (i + 1) * tile, :]
    state_dims = (((1,), (1 if swap else 0,)), ((), ()))
    by_key = [None] * count
    per = pieces // count
    for i in range(count):
        q_i, g_i, col_i = cut(q, i), cut(g, i), cut(col, i)
        wide = jnp.concatenate([col_i] * (tile // width), axis=1)
        q_start = (q_i.astype(f32) * jnp.exp(col_i)).astype(bf16)
        acc = scaling * lax.dot_general(q_start, in_ref[...], state_dims, preferred_element_type=f32)
        for j in range(i + 1):
            s = lax.dot_general(q_i, cut(k, j), (((1,), (1,)), ((), ())), preferred_element_type=f32)
            gap = wide - row[:, j * tile : (j + 1) * tile]
            if i == j:
                keep = lax.broadcasted_iota(jnp.int32, (tile, tile), 0) >= lax.broadcasted_iota(
                    jnp.int32, (tile, tile), 1
                )
                decay = jnp.where(keep, jnp.exp(jnp.where(keep, gap, 0.0)), 0.0)
            else:
                decay = jnp.exp(gap)
            w = (scaling * s * decay).astype(bf16)
            acc = acc + lax.dot_general(w, cut(v, j), (((1,), (0,)), ((), ())), preferred_element_type=f32)
            back = lax.dot_general(w, g_i, (((0,), (0,)), ((), ())), preferred_element_type=f32)
            by_key[j] = back if by_key[j] is None else by_key[j] + back
        o_ref[i * per : (i + 1) * per, 0] = acc.astype(bf16).reshape(per, -1, width)
    for j in range(count):
        k_end = (cut(k, j).astype(f32) * jnp.exp(total - cut(col, j))).astype(bf16)
        acc = by_key[j] + scaling * lax.dot_general(
            k_end, out_ref[...], state_dims, preferred_element_type=f32
        )
        o_ref[j * per : (j + 1) * per, 1] = acc.astype(bf16).reshape(per, -1, width)


def shards(query_in, key_in, value_in, grad_out, log_decay):
    tokens, all_heads, width = query_in.shape
    groups = lax.axis_size("head")
    heads = all_heads // groups
    segs = lax.axis_size("seq")
    length = tokens * groups

    def scatter_heads(a, b):
        pair = jnp.stack([a, b]).reshape(2, tokens, groups, heads, width).transpose(2, 0, 3, 1, 4)
        return lax.all_to_all(pair, "head", split_axis=0, concat_axis=0, tiled=True)

    decays = log_decay.reshape(tokens, groups, heads).transpose(1, 2, 0)
    decays = lax.all_to_all(decays, "head", split_axis=0, concat_axis=0, tiled=True)
    within = jnp.cumsum(decays.astype(f32).transpose(1, 0, 2).reshape(heads, length), axis=1)
    totals = lax.all_to_all(
        jnp.broadcast_to(within[None, :, -1], (segs, heads)), "seq", split_axis=0, concat_axis=0, tiled=True
    )
    within = within[:, None, :]
    kv_in = scatter_heads(key_in, value_in)
    qg_in = scatter_heads(query_in, grad_out)

    cum_inc = jnp.cumsum(totals, axis=0)
    cum_exc = cum_inc - totals
    ranks = jnp.arange(segs)
    earlier = (ranks[None, :] < ranks[:, None])[:, :, None]
    later_on = (ranks[None, :] > ranks[:, None])[:, :, None]
    w_in = jnp.where(
        earlier, jnp.exp(jnp.where(earlier, cum_exc[:, None, :] - cum_inc[None, :, :], 0.0)), 0.0
    )
    w_out = jnp.where(
        later_on, jnp.exp(jnp.where(later_on, cum_exc[None, :, :] - cum_inc[:, None, :], 0.0)), 0.0
    )
    weights = jnp.stack([w_in, w_out]).transpose(0, 3, 1, 2)

    def part(which):
        return pl.BlockSpec((groups, None, None, tokens, width), lambda h: (0, which, h, 0, 0))

    row = pl.BlockSpec((None, 1, length), lambda h: (h, 0, 0))
    square = pl.BlockSpec((None, width, width), lambda h: (h, 0, 0))
    state = jax.ShapeDtypeStruct((heads, width, width), bf16)
    local_kv, local_qg = pl.pallas_call(
        local_states_kernel,
        grid=(heads,),
        in_specs=[part(0), part(0), part(1), part(1), row],
        out_specs=[square, square],
        out_shape=[state, state],
    )(qg_in, kv_in, kv_in, qg_in, within)

    rows = width // segs
    local = jnp.stack([local_kv, local_qg]).reshape(2, heads, segs, rows * width).transpose(2, 0, 1, 3)
    gathered = lax.all_to_all(local, "seq", split_axis=0, concat_axis=0, tiled=True)
    states = jnp.einsum("chji,ichr->jchr", weights, gathered.astype(f32), precision=precise).astype(bf16)
    states = lax.all_to_all(states, "seq", split_axis=0, concat_axis=0, tiled=True)
    states = states.transpose(1, 2, 0, 3).reshape(2, heads, width, width)

    def attention(swap, q, k, v, g):
        return pl.pallas_call(
            functools.partial(attention_kernel, swap, min(256, length)),
            grid=(heads,),
            in_specs=[
                part(q[1]), part(k[1]), part(v[1]), part(g[1]), row,
                pl.BlockSpec((None, None, width, width), lambda h: (0, h, 0, 0)),
                pl.BlockSpec((None, None, width, width), lambda h: (1, h, 0, 0)),
            ],
            out_specs=pl.BlockSpec((groups, 2, None, tokens, width), lambda h: (0, 0, h, 0, 0)),
            out_shape=jax.ShapeDtypeStruct((groups, 2, heads, tokens, width), bf16),
            cost_estimate=pl.CostEstimate(
                flops=6 * heads * length * length * width,
                bytes_accessed=12 * heads * length * width,
                transcendentals=heads * length * length // 2,
            ),
        )(q[0], k[0], v[0], g[0], within, states, states)

    queries, grads, keys, values = (qg_in, 0), (qg_in, 1), (kv_in, 0), (kv_in, 1)
    first = attention(False, queries, keys, values, grads)
    second = attention(True, grads, values, keys, queries)

    def gather_heads(pair):
        pair = lax.all_to_all(pair, "head", split_axis=0, concat_axis=0, tiled=True)
        pair = pair.transpose(1, 3, 0, 2, 4).reshape(2, tokens, all_heads, width)
        return pair[0], pair[1]

    attended, grad_value = gather_heads(first)
    grad_query, grad_key = gather_heads(second)
    return attended, grad_query, grad_key, grad_value


def solution(mesh):
    tall = P(("seq", "head"), None, None)
    return jax.shard_map(
        shards,
        mesh=mesh,
        in_specs=(tall, tall, tall, tall, P(("seq", "head"), None)),
        out_specs=(tall, tall, tall, tall),
        check_vma=False,
    )
```
